32 devices in a mesh: fsdp: 8 (over z, y), ctx: 2 (over x), tp: 2 (over core).
Axes of the slice: x: 2, y: 2, z: 4, core: 2. Of those that a mesh axis runs over, the one named last changes fastest.
Arguments:
- inputs: bfloat16 [2, 16, 592, 1024], P(None, ('fsdp', 'tp'), 'ctx'), may hold values from -6 to 6
- cotangent: bfloat16 [2, 16, 592, 1024], P(None, ('fsdp', 'tp'), 'ctx'), may hold values from -6 to 6
- slot_mask: int32 [2, 16], P(None, ('fsdp', 'tp')), may hold values 0 or 1
- key_mask: int32 [2, 16, 592], P(None, 'fsdp'), may hold values from 0 to 1, as said below
- ln1_gain: bfloat16 [1024], P('fsdp'), may hold values from 0.5 to 1.5
- ln1_bias: bfloat16 [1024], P('fsdp'), may hold values from -0.796875 to 0.796875
- w_qkv: bfloat16 [1024, 3, 1024], P('fsdp', None, 'tp'), may hold values from -0.1875 to 0.1875
- b_qv: bfloat16 [2, 16, 64], P(None, 'tp', 'fsdp'), may hold values from -0.796875 to 0.796875
- w_out: bfloat16 [1024, 1024], P('tp', 'fsdp'), may hold values from -2.5 to 2.5
- b_out: bfloat16 [1024], P('fsdp'), may hold values from -0.796875 to 0.796875
- ln2_gain: bfloat16 [1024], P('fsdp'), may hold values from 0.5 to 1.5
- ln2_bias: bfloat16 [1024], P('fsdp'), may hold values from -0.796875 to 0.796875
- w_fc1: bfloat16 [1024, 4096], P('fsdp', 'tp'), may hold values from -0.1875 to 0.1875
- b_fc1: bfloat16 [64, 64], P('tp', 'fsdp'), may hold values from -0.796875 to 0.796875
- w_fc2: bfloat16 [4096, 1024], P('tp', 'fsdp'), may hold values from -0.09375 to 0.09375
- b_fc2: bfloat16 [1024], P('fsdp'), may hold values from -0.796875 to 0.796875
Outputs:
- outputs: bfloat16 [2, 16, 592, 1024], P(None, ('fsdp', 'tp'), 'ctx')
- input_grad: bfloat16 [2, 16, 592, 1024], P(None, ('fsdp', 'tp'), 'ctx')
- ln1_gain_grad: float32 [1024], P(('fsdp', 'ctx', 'tp'))
- ln1_bias_grad: float32 [1024], P(('fsdp', 'ctx', 'tp'))
- w_qkv_grad: float32 [1024, 3, 1024], P(('fsdp', 'ctx'), None, 'tp')
- b_qv_grad: float32 [2, 16, 64], P(None, 'tp', ('fsdp', 'ctx'))
- w_out_grad: float32 [1024, 1024], P('tp', ('fsdp', 'ctx'))
- b_out_grad: float32 [1024], P(('fsdp', 'ctx', 'tp'))
- ln2_gain_grad: float32 [1024], P(('fsdp', 'ctx', 'tp'))
- ln2_bias_grad: float32 [1024], P(('fsdp', 'ctx', 'tp'))
- w_fc1_grad: float32 [1024, 4096], P(('fsdp', 'ctx'), 'tp')
- b_fc1_grad: float32 [64, 64], P('tp', ('fsdp', 'ctx'))
- w_fc2_grad: float32 [4096, 1024], P('tp', ('fsdp', 'ctx'))
- b_fc2_grad: float32 [1024], P(('fsdp', 'ctx', 'tp'))
The draws below stay inside these ranges and needn't reach their ends.
Inputs may be any that keep to these rules, and one draw needn't show every extreme that they name: `key_mask`: position 0 of every image is 1; positions 577 and beyond are 0.
All inputs are finite; a program needn't handle non-finite values. No bound on the sum of `slot_mask` on one device may be relied on, other than what follows from the above.
Results may differ from the reference program's by a relative error of at most 0.023.
Values may be sent and summed in bfloat16 or wider, within the bound.
A program may use at most 256 MiB of HBM per device.

```python
import jax
import jax.numpy as jnp
from jax import lax

D = 1024
HEADS = 16
HD = 64
FF = 4096
SEQ_LEN = 577
MICRO = 2
SEQP = 592
IMAGES = 16
N_FSDP = 8


def draw_key_mask(key, part):
    keep_draw = jax.random.randint(key, (MICRO, IMAGES, SEQP), 0, 8) > 0
    position = jnp.arange(SEQP)
    valid_keys = (position < SEQ_LEN)[None, None, :] & (keep_draw | (position == 0)[None, None, :])
    return valid_keys.astype(jnp.int32)


def plant(entries, rng, least, top_value):
    extent = entries.shape
    place = [jax.random.randint(jax.random.fold_in(rng, axis), (), 0, extent[axis]) for axis in range(len(extent))]
    entries = entries.at[tuple(place)].set(least)
    longest = extent.index(max(extent))
    place[longest] = (place[longest] + 1) % extent[longest]
    return entries.at[tuple(place)].set(top_value)


def strengthened(values, stream_key, source, target, shards_of, factor):
    def block_of(axis_at):
        return (jnp.arange(values.shape[axis_at]) // (values.shape[axis_at] // shards_of)).reshape((-1,) + (1,) * (values.ndim - 1 - axis_at))

    near = jax.random.permutation(stream_key, shards_of)[block_of(target)]
    second = (block_of(target) + shards_of // 2) % shards_of
    return jnp.where((block_of(source) == near) | (block_of(source) == second), factor * values, values)


def level_of(key, extent, cuts, low, high):
    gain, own = 1.0, jax.random.fold_in(key, 6)
    for axis_at, blocks in cuts:
        steps = jnp.exp(jax.random.uniform(jax.random.fold_in(own, axis_at), (blocks,), jnp.float32, low / len(cuts), high / len(cuts)))
        gain = gain * jnp.repeat(steps, extent[axis_at] // blocks).reshape([-1 if axis == axis_at else 1 for axis in range(len(extent))])
    return gain


def noise(key, shape, deviation, limit, split=(), held_as=jnp.bfloat16):
    values = deviation * jax.random.normal(key, shape, jnp.float32)
    if split:
        values = values * level_of(key, shape, split, -0.22, 0.18)
    return jnp.clip(values, -limit, limit).astype(held_as)


def heavy_noise(own_key, dims, width, limit, cuts, heavy, kind=jnp.bfloat16):
    values = width * jax.random.normal(own_key, dims, jnp.float32)
    if cuts:
        values = values * level_of(own_key, dims, cuts, -0.22, 0.18)
    return jnp.clip(strengthened(values, jax.random.fold_in(own_key, 3), *heavy), -limit, limit).astype(kind)


def setup_inputs(seed: int = 0) -> dict:
    streams_of = jax.random.split(jax.random.key(seed), 17)
    inputs = noise(streams_of[0], (MICRO, IMAGES, SEQP, D), 1.0, 6.0, ((1, 16), (2, 2)))
    cotangent = heavy_noise(streams_of[1], (MICRO, IMAGES, SEQP, D), 1.0, 6.0, ((1, 16), (2, 2)), (1, 3, 16, 2.0))
    slot_mask = plant((jax.random.randint(streams_of[2], (MICRO, IMAGES), 0, 4) < 3).astype(jnp.int32), jax.random.fold_in(streams_of[2], 1), 0, 1)
    key_mask = draw_key_mask(jax.random.fold_in(streams_of[16], 71), 0)
    ln1_gain = jnp.clip(1.0 + 0.1 * jax.random.normal(streams_of[4], (D,), jnp.float32), 0.5, 1.5).astype(jnp.bfloat16)
    ln1_bias = noise(streams_of[5], (D,), 0.2, 0.796875, ((0, 8),))
    w_qkv = noise(streams_of[6], (D, 3, D), D ** -0.5, 0.1875, ((0, 8), (2, 2)))
    b_qv = noise(streams_of[7], (2, HEADS, HD), 0.2, 0.796875, ((1, 2), (2, 8)))
    w_out = noise(streams_of[8], (D, D), 6 ** -0.5, 2.5, ((0, 2), (1, 8)))
    b_out = noise(streams_of[9], (D,), 0.2, 0.796875, ((0, 8),))
    ln2_gain = jnp.clip(1.0 + 0.1 * jax.random.normal(streams_of[10], (D,), jnp.float32), 0.5, 1.5).astype(jnp.bfloat16)
    ln2_bias = noise(streams_of[11], (D,), 0.2, 0.796875, ((0, 8),))
    w_fc1 = noise(streams_of[12], (D, FF), D ** -0.5, 0.1875, ((0, 8), (1, 2)))
    b_fc1 = noise(streams_of[13], (FF // 64, 64), 0.2, 0.796875, ((0, 2), (1, 8)))
    w_fc2 = noise(streams_of[14], (FF, D), FF ** -0.5, 0.09375, ((0, 2), (1, 8)))
    b_fc2 = noise(streams_of[15], (D,), 0.2, 0.796875, ((0, 8),))
    return {"inputs": inputs, "cotangent": cotangent, "slot_mask": slot_mask, "key_mask": key_mask, "ln1_gain": ln1_gain, "ln1_bias": ln1_bias, "w_qkv": w_qkv, "b_qv": b_qv, "w_out": w_out, "b_out": b_out, "ln2_gain": ln2_gain, "ln2_bias": ln2_bias, "w_fc1": w_fc1, "b_fc1": b_fc1, "w_fc2": w_fc2, "b_fc2": b_fc2}


@jax.custom_vjp
def low(v):
    return lax.optimization_barrier(v.astype(jnp.bfloat16)).astype(jnp.float32)

@jax.custom_vjp
def low_back(v):
    return v

def low_keep(v):
    return (low(v), None)

def low_pass(kept, grad):
    return (grad,)

def back_keep(v):
    return (v, None)

def back_low(kept, grad):
    return (low(grad),)
low.defvjp(low_keep, low_pass)
low_back.defvjp(back_keep, back_low)

def normalize(values, gain_row, shift_row):
    average = lax.optimization_barrier(jnp.mean(values, axis=-1, keepdims=True))
    centred = values - average
    inv_std = lax.rsqrt(lax.optimization_barrier(jnp.mean(centred * centred, axis=-1, keepdims=True)) + 1e-05)
    return centred * inv_std * gain_row + shift_row

def matmul(left_side, right_side):
    return jnp.dot(left_side, right_side, precision=lax.Precision.HIGHEST)

def layer(block_in, params, key_valid, row_valid):
    ln1_gain, ln1_bias, w_qkv, b_qv, w_out, b_out, ln2_gain, ln2_bias, w_fc1, b_fc1, w_fc2, b_fc2 = params
    image_count, seq_count, model_width = block_in.shape
    rows_in = block_in.reshape(image_count * seq_count, model_width)
    normed_one = low(normalize(rows_in, ln1_gain, ln1_bias))
    joint_proj = matmul(normed_one, w_qkv.reshape(model_width, 3 * model_width))
    joint_proj = joint_proj.reshape(image_count, seq_count, 3, HEADS, HD)
    query_all = low(low_back(joint_proj[:, :, 0] + b_qv[0]))
    keys_all = low(low_back(joint_proj[:, :, 1]))
    values_all = low(low_back(joint_proj[:, :, 2] + b_qv[1]))
    scores = jnp.einsum('gqhd,gkhd->ghqk', query_all, keys_all, precision=lax.Precision.HIGHEST) * 0.125
    scores = low_back(jnp.where(key_valid[:, None, None, :] > 0, scores, -jnp.inf))
    soft_low = low(jax.nn.softmax(scores, axis=-1))
    mixed_heads = jnp.einsum('ghqk,gkhd->gqhd', soft_low, values_all, precision=lax.Precision.HIGHEST)
    mixed_heads = low(low_back(mixed_heads.reshape(image_count * seq_count, model_width)))
    hidden_one = rows_in + low_back(matmul(mixed_heads, w_out)) + b_out
    normed_two = low(normalize(hidden_one, ln2_gain, ln2_bias))
    before = low_back(matmul(normed_two, w_fc1) + b_fc1.reshape(-1))
    active = low(before * jax.nn.sigmoid(1.702 * before))
    result = hidden_one + low_back(matmul(active, w_fc2)) + b_fc2
    return result.reshape(image_count, seq_count, model_width) * row_valid[:, :, None]

def reference(inputs, cotangent, slot_mask, key_mask, ln1_gain, ln1_bias, w_qkv, b_qv, w_out, b_out, ln2_gain, ln2_bias, w_fc1, b_fc1, w_fc2, b_fc2):
    params = tuple((weight.astype(jnp.float32) for weight in (ln1_gain, ln1_bias, w_qkv, b_qv, w_out, b_out, ln2_gain, ln2_bias, w_fc1, b_fc1, w_fc2, b_fc2)))
    group_size = IMAGES // N_FSDP
    blocks = MICRO * N_FSDP
    position_ok = jnp.arange(SEQP) < SEQ_LEN
    row_valid = ((slot_mask > 0)[:, :, None] & position_ok[None, None, :]).astype(jnp.float32)

    def to_blocks(array):
        return array.reshape((blocks, group_size) + array.shape[2:])

    def one_block(totals, pieces):
        block_in, block_cot, block_keys, block_rows = pieces

        def forward(values, weights):
            return layer(values, weights, block_keys, block_rows)
        result, pullback = jax.vjp(forward, block_in.astype(jnp.float32), params)
        grad_in, param_grads = pullback(block_cot.astype(jnp.float32))
        totals = jax.tree.map(lambda left_side, right_side: left_side + right_side, totals, param_grads)
        return (totals, (result.astype(jnp.bfloat16), grad_in.astype(jnp.bfloat16)))
    zeros = jax.tree.map(jnp.zeros_like, params)
    totals, (outputs, input_grad) = lax.scan(one_block, zeros, (to_blocks(inputs), to_blocks(cotangent), to_blocks(key_mask), to_blocks(row_valid)))
    full_shape = inputs.shape
    return (outputs.reshape(full_shape), input_grad.reshape(full_shape), totals[0], totals[1], totals[2], totals[3], totals[4], totals[5], totals[6], totals[7], totals[8], totals[9], totals[10], totals[11])
```

```python
import functools
import jax
import jax.numpy as jnp
from jax import lax
from jax.experimental import pallas as pl
from jax.experimental.pallas import tpu as pltpu
from jax.sharding import PartitionSpec as P

MESH = pl.DeviceIdType.MESH
BF = jnp.bfloat16
F32 = jnp.float32


class Place:
    def __init__(self, fsdp, ctx, tp):
        self.count, self.lines, self.tp_size = fsdp, fsdp // 2, tp
        self.fsdp = lax.axis_index("fsdp")
        self.line, self.pair = self.fsdp // 2, self.fsdp % 2
        self.half = lax.axis_index("ctx")
        self.core = lax.axis_index("tp")
        self.to_pair = {"fsdp": self.line * 2 + (1 - self.pair)}
        self.to_half = {"ctx": 1 - self.half}
        self.to_up = {"fsdp": self.fsdp + 2}
        self.to_down = {"fsdp": self.fsdp - 2}
        self.has_up = self.line < self.lines - 1
        self.has_down = self.line > 0

    def to_line(self, step):
        return {"fsdp": lax.rem(self.line + step, self.lines) * 2 + self.pair}

    def to_core(self, step):
        return {"tp": lax.rem(self.core + step, self.tp_size)}


def copy_to(src, dst, sems, slot, target):
    return pltpu.make_async_remote_copy(
        src_ref=src,
        dst_ref=dst,
        send_sem=sems[0].at[slot],
        recv_sem=sems[1].at[slot],
        device_id=target,
        device_id_type=MESH,
    )


def when(condition, action):
    if condition is True:
        action()
    else:
        pl.when(condition)(action)


class Gather:
    def __init__(self, place, pieces, sems, local_sems):
        self.place, self.pieces, self.sems, self.local_sems = place, pieces, sems, local_sems
        lines = place.lines
        names = ["first"]
        for kind in ("up", "down", "up_half", "down_half", "single_up", "single_down"):
            names += [(kind, step) for step in range(1, lines)]
        for kind in ("up_far", "down_far", "up_pair", "down_pair"):
            names += [(kind, step) for step in range(1, lines)]
        names += ["own_half", "own_pair", "up0a", "up0b", "down0a", "down0b"]
        names += [("core", step) for step in range(1, place.tp_size)]
        self.names = {name: number for number, name in enumerate(names)}
        self.width = len(names)
        self.pending = []

    @staticmethod
    def slots(lines, tp):
        return 1 + 10 * (lines - 1) + 6 + tp - 1

    def slot(self, piece, name):
        return piece * self.width + self.names[name]

    def whole(self, piece, core, line=slice(None), pair=slice(None), half=slice(None), color=slice(None)):
        _, ref, offset, width, per_core = self.pieces[piece]
        columns = pl.ds(pl.multiple_of(core * per_core + offset, 128), width)
        index = (line, pair, half, color, slice(None), columns)
        return ref.at[(slice(None),) * (len(ref.shape) - 6) + index]

    def own(self, piece, half=slice(None), color=slice(None)):
        ref, _, offset, width, _ = self.pieces[piece]
        index = (half, color, slice(None), pl.ds(offset, width))
        return ref.at[(slice(None),) * (len(ref.shape) - 4) + index]

    def send(self, piece, name, src, dst, target, condition=True):
        copy = copy_to(src, dst, self.sems, self.slot(piece, name), target)
        when(condition, copy.start)
        self.pending.append((copy, condition))

    def arrive(self, piece, name, dst, condition=True):
        copy = copy_to(dst, dst, self.sems, self.slot(piece, name), self.place.to_half)
        when(condition, copy.wait_recv)

    def local(self, piece):
        me = self.place
        return pltpu.make_async_copy(
            self.own(piece), self.whole(piece, me.core, me.line, me.pair), self.local_sems.at[piece]
        )

    def stage(self, p, k):
        me = self.place
        core, line, pair, half = me.core, me.line, me.pair, me.half
        lines = me.lines
        view = functools.partial(self.whole, p, core)
        if k == 0:
            self.local(p).start()
            self.send(p, "first", self.own(p, half, 0), view(line, pair, half, 0), me.to_pair)
            self.send(p, ("single_up", 1), self.own(p, half, 1), view(line, pair, half, 1), me.to_up, me.has_up)
            self.send(p, ("single_down", 1), self.own(p, half, 1), view(line, pair, half, 1), me.to_down, me.has_down)
            self.send(p, "up0a", self.own(p, half, 0), view(line, pair, half, 0), me.to_up, me.has_up)
            self.send(p, "down0a", self.own(p, half, 0), view(line, pair, half, 0), me.to_down, me.has_down)
            self.send(p, "own_pair", self.own(p, slice(None), 1), view(line, pair, slice(None), 1), me.to_pair)
        if k == 1:
            other = view(line, 1 - pair, half, 0)
            self.arrive(p, "first", other)
            self.send(p, "up0b", other, other, me.to_up, me.has_up)
            self.send(p, "down0b", other, other, me.to_down, me.has_down)
            self.send(p, "own_half", other, other, me.to_half)
        if 1 <= k < lines:
            for sign, kind, target, more, enough in (
                (-1, "up", me.to_up, me.has_up, line >= k),
                (1, "down", me.to_down, me.has_down, line < lines - k),
            ):
                source = line + sign * k
                item = view(source, pair, half, 1)
                self.arrive(p, ("single_" + kind, k), item, enough)
                if k + 1 < lines:
                    self.send(p, ("single_" + kind, k + 1), item, item, target, enough & more)
                self.send(p, (kind + "_half", k), item, item, me.to_half, enough)
        if 2 <= k <= lines:
            step = k - 1
            for sign, kind, target, more, enough in (
                (-1, "up", me.to_up, me.has_up, line >= step),
                (1, "down", me.to_down, me.has_down, line < lines - step),
            ):
                source = line + sign * step
                both = view(source, slice(None), half, 0)
                if step == 1:
                    self.arrive(p, kind + "0a", view(source, pair, half, 0), enough)
                    self.arrive(p, kind + "0b", view(source, 1 - pair, half, 0), enough)
                else:
                    self.arrive(p, (kind, step), both, enough)
                if step + 1 < lines:
                    self.send(p, (kind, step + 1), both, both, target, enough & more)
                self.send(p, (kind + "_far", step), both, both, me.to_half, enough)
                self.arrive(p, (kind + "_half", step), view(source, pair, 1 - half, 1), enough)
                item = view(source, pair, slice(None), 1)
                self.send(p, (kind + "_pair", step), item, item, me.to_pair, enough)
        if k == lines + 1:
            self.arrive(p, "own_half", view(line, 1 - pair, 1 - half, 0))
            self.arrive(p, "own_pair", view(line, 1 - pair, slice(None), 1))
            for step in range(1, lines):
                for sign, kind, enough in ((-1, "up", line >= step), (1, "down", line < lines - step)):
                    source = line + sign * step
                    self.arrive(p, (kind + "_far", step), view(source, slice(None), 1 - half, 0), enough)
                    self.arrive(p, (kind + "_pair", step), view(source, 1 - pair, slice(None), 1), enough)
            self.local(p).wait()
            for step in range(1, me.tp_size):
                self.send(p, ("core", step), view(), view(), me.to_core(step))
        if k == lines + 2:
            for step in range(1, me.tp_size):
                sender = lax.rem(core - step + me.tp_size, me.tp_size)
                self.arrive(p, ("core", step), self.whole(p, sender))

    def stages(self):
        return self.place.lines + 3

    def finish(self):
        for copy, condition in self.pending:
            when(condition, copy.wait_send)


def greet_all(place):
    barrier = pltpu.get_barrier_semaphore()
    targets = [place.to_pair, place.to_half]
    targets += [place.to_core(step) for step in range(1, place.tp_size)]
    targets += [place.to_line(step) for step in range(1, place.lines)]
    for target in targets:
        pl.semaphore_signal(barrier, inc=1, device_id=target, device_id_type=MESH)
    pl.semaphore_wait(barrier, len(targets))


class Small:
    def __init__(self, place, own, whole, sems, slot):
        self.place, self.own, self.whole, self.sems, self.slot = place, own, whole, sems, slot
        self.copies = []

    def stage(self, k):
        me = self.place
        for copy in self.copies:
            copy.wait()
        first, targets, block = {
            0: (0, [me.to_pair], self.whole.at[me.core, me.fsdp]),
            1: (1, [me.to_line(step) for step in range(1, me.lines)], self.whole.at[me.core, pl.ds(me.line * 2, 2)]),
            2: (me.lines, [me.to_core(step) for step in range(1, me.tp_size)], self.whole.at[me.core]),
            3: (0, [], None),
        }[k]
        if k == 0:
            block[...] = self.own[...]
        self.copies = []
        for number, target in enumerate(targets):
            copy = copy_to(block, block, self.sems, self.slot + first + number, target)
            copy.start()
            self.copies.append(copy)


def gather_kernel(sizes, *refs):
    shards, (tokens, cotangent, small), refs = refs[:4], refs[4:7], refs[7:]
    wholes, (all_tokens, all_cotangent, all_small), refs = refs[:4], refs[4:7], refs[7:]
    send, recv, local_sems = refs
    place = Place(*sizes)
    greet_all(place)
    pieces = []
    for g, part, parts in ((0, 0, 1), (1, 0, 1), (2, 0, 2), (2, 1, 2), (3, 0, 2), (3, 1, 2)):
        per_core = shards[g].shape[-1]
        width = per_core // parts
        pieces.append((shards[g], wholes[g], part * width, width, per_core))
    gather = Gather(place, pieces, (send, recv), local_sems)
    extra = len(pieces) * gather.width
    small_gather = Small(place, small, all_small, (send, recv), extra + 2)
    exchanges = []
    half = place.half
    for number, (own, whole) in enumerate(((tokens, all_tokens), (cotangent, all_cotangent))):
        exchanges.append(copy_to(own.at[1 - half], whole.at[half], (send, recv), extra + number, place.to_half))
        exchanges.append(pltpu.make_async_copy(own.at[half], whole.at[half], local_sems.at[len(pieces) + number]))
    for slot in range(len(pieces) + gather.stages() - 1):
        for p in range(len(pieces)):
            if 0 <= slot - p < gather.stages():
                gather.stage(p, slot - p)
        if slot < 4:
            small_gather.stage(slot)
        if slot == 0:
            for copy in exchanges:
                copy.start()
    for copy in exchanges:
        copy.wait()
    gather.finish()


def gather_all(mesh, shards, tokens, cotangent, small):
    fsdp, ctx, tp = (mesh.shape[name] for name in ("fsdp", "ctx", "tp"))
    lines = fsdp // 2
    rows = shards[2].shape[0] // 4

    def split(shard):
        return shard.reshape(shard.shape[:-2] + (2, 2, rows, shard.shape[-1]))

    shards = [split(shard) for shard in shards]

    def whole(shard):
        return jax.ShapeDtypeStruct(shard.shape[:-4] + (lines, 2, 2, 2, rows, shard.shape[-1] * tp), BF)

    arrivals = 2 + 1 + lines - 1 + tp - 1
    count = 6 * Gather.slots(lines, tp) + arrivals
    vmem, hbm = pl.BlockSpec(memory_space=pltpu.VMEM), pl.BlockSpec(memory_space=pl.ANY)
    found = pl.pallas_call(
        functools.partial(gather_kernel, (fsdp, ctx, tp)),
        name="gather_weights",
        out_shape=[whole(shard) for shard in shards]
        + [jax.ShapeDtypeStruct(tokens.shape, BF)] * 2
        + [jax.ShapeDtypeStruct((tp, fsdp) + small.shape, small.dtype)],
        in_specs=[vmem] * 7,
        out_specs=[hbm] * 6 + [vmem],
        scratch_shapes=[
            pltpu.SemaphoreType.DMA((count,)),
            pltpu.SemaphoreType.DMA((count,)),
            pltpu.SemaphoreType.DMA((8,)),
        ],
        compiler_params=pltpu.CompilerParams(collective_id=0, has_side_effects=True),
    )(*shards, tokens, cotangent, small)
    return [one.reshape(one.shape[:-6] + (rows * 4 * fsdp, one.shape[-1])) for one in found[:4]] + list(found[4:])


class Scatter:
    KINDS = ("half0", "pair1", "half1", "pair0")

    def __init__(self, place, pieces, sems, local_sems):
        self.place, self.pieces, self.sems, self.local_sems = place, pieces, sems, local_sems
        lines = place.lines
        names = list(self.KINDS)
        for kind in ("up0", "down0", "up1", "down1"):
            names += [(kind, step) for step in range(1, lines)]
        names += [("core", step) for step in range(1, place.tp_size)]
        self.names = {name: number for number, name in enumerate(names)}
        self.width = len(names)
        self.pending = []

    @staticmethod
    def slots(lines, tp):
        return 4 + 4 * (lines - 1) + tp - 1

    @staticmethod
    def buffers(lead, lines, tp, rows, width):
        block = (rows, width)
        return [
            pltpu.VMEM((lead, lines, 2, 2, 2) + block, BF),
            pltpu.VMEM((tp - 1, lead, lines, 2, 2, 2) + block, BF),
            pltpu.VMEM((lead, lines, 2) + block, BF),
            pltpu.VMEM((lead, lines, 2) + block, BF),
            pltpu.VMEM((lead, lines) + block, BF),
            pltpu.VMEM((lead,) + block, BF),
            pltpu.VMEM((2, lines - 1, lead, 2) + block, BF),
            pltpu.VMEM((2, lines - 1, lead) + block, BF),
        ]

    def slot(self, piece, name):
        return piece * self.width + self.names[name]

    def send(self, piece, name, src, dst, target, condition=True):
        copy = copy_to(src, dst, self.sems, self.slot(piece, name), target)
        when(condition, copy.start)
        self.pending.append((copy, condition))

    def arrive(self, piece, name, dst, condition=True):
        copy = copy_to(dst, dst, self.sems, self.slot(piece, name), self.place.to_half)
        when(condition, copy.wait_recv)

    def add(self, sizes, into, found, condition=True):
        count = 1
        for size in sizes:
            count *= size

        def one(number, _):
            index = []
            for size in reversed(sizes):
                index.append(lax.rem(number, size))
                number = number // size
            index = tuple(reversed(index))
            here, there = into(*index), found(*index)
            here[...] = here[...] + there[...]
            return 0

        def run():
            lax.fori_loop(0, count, one, 0)

        when(condition, run)

    def grads(self, piece, core):
        grad, offset, width, per_core = self.pieces[piece][:4]
        columns = pl.ds(pl.multiple_of(core * per_core + offset, 128), width)
        return grad.at[(slice(None),) * (len(grad.shape) - 1) + (columns,)]

    def local(self, piece):
        total = self.pieces[piece][5]
        return pltpu.make_async_copy(self.grads(piece, self.place.core), total, self.local_sems.at[piece])

    def stage(self, p, k):
        me = self.place
        core, line, pair, half, lines = me.core, me.line, me.pair, me.half, me.lines
        out, total, cores, half0, pair1, half1, pair0, line0, line1 = self.pieces[p][4:]
        lead = total.shape[0]
        every = slice(None)
        if k == 0:
            self.local(p).start()
            for step in range(1, me.tp_size):
                target = lax.rem(core + step, me.tp_size)
                self.send(p, ("core", step), self.grads(p, target), cores.at[step - 1], me.to_core(step))
        if k == 1:
            self.local(p).wait()
            for step in range(1, me.tp_size):
                self.arrive(p, ("core", step), cores.at[step - 1])
                self.add(
                    (lead, lines, 2, 2, 2),
                    lambda *i: total.at[i],
                    lambda *i, step=step: cores.at[(step - 1,) + i],
                )
            self.send(p, "half0", total.at[:, :, :, 1 - half, 0], half0, me.to_half)
            self.send(p, "pair1", total.at[:, :, 1 - pair, :, 1], pair1, me.to_pair)
        if k == 2:
            self.arrive(p, "half0", half0)
            self.add((lead, lines, 2), lambda l, n, q: total.at[l, n, q, half, 0], lambda *i: half0.at[i])
            self.arrive(p, "pair1", pair1)
            self.add((lead, lines, 2), lambda l, n, q: total.at[l, n, pair, q, 1], lambda *i: pair1.at[i])
            self.send(p, "half1", total.at[:, :, pair, 1 - half, 1], half1, me.to_half)
        if k == 3:
            self.arrive(p, "half1", half1)
            self.add((lead, lines), lambda l, n: total.at[l, n, pair, half, 1], lambda *i: half1.at[i])
        for color, first, buffer in ((0, 2, line0), (1, 3, line1)):
            distance = lines - 1 - (k - first)
            if 1 <= distance + 1 <= lines - 1:
                d = distance + 1
                for way, sign, kind, enough in (
                    (0, -1, "up", (line >= 1) & (line - 1 + d < lines)),
                    (1, 1, "down", (line < lines - 1) & (line + 1 - d >= 0)),
                ):
                    about = line + sign - sign * d
                    self.arrive(p, (kind + str(color), d), buffer.at[way, d - 1], enough)
                    if color == 0:
                        self.add(
                            (lead, 2),
                            lambda l, q, about=about: total.at[l, about, q, half, 0],
                            lambda l, q, way=way, d=d: line0.at[way, d - 1, l, q],
                            enough,
                        )
                    else:
                        self.add(
                            (lead,),
                            lambda l, about=about: total.at[l, about, pair, half, 1],
                            lambda l, way=way, d=d: line1.at[way, d - 1, l],
                            enough,
                        )
            if 1 <= distance <= lines - 1:
                d = distance
                for way, sign, kind, target, enough in (
                    (0, -1, "up", me.to_up, line + d < lines),
                    (1, 1, "down", me.to_down, line - d >= 0),
                ):
                    about = line - sign * d
                    src = total.at[:, about, :, half, 0] if color == 0 else total.at[:, about, pair, half, 1]
                    self.send(p, (kind + str(color), d), src, buffer.at[way, d - 1], target, enough)
        if k == lines + 1:
            self.send(p, "pair0", total.at[:, line, 1 - pair, half, 0], pair0, me.to_pair)
        if k == lines + 2:
            self.arrive(p, "pair0", pair0)
            for l in range(lead):
                out[l, 0] = total[l, line, pair, half, 0].astype(F32) + pair0[l].astype(F32)
                out[l, 1] = total[l, line, pair, half, 1].astype(F32)

    def stages(self):
        return self.place.lines + 3

    def finish(self):
        for copy, condition in self.pending:
            when(condition, copy.wait_send)


def all_sum(place, values, buffers, sems, slot):
    pending = []

    def send(number, target, condition=True):
        copy = copy_to(values, buffers.at[number], sems, slot + number, target)
        when(condition, copy.start)
        return copy

    number = 0
    for targets in (
        [place.to_core(step) for step in range(1, place.tp_size)],
        [place.to_half],
        [place.to_pair],
        [place.to_line(step) for step in range(1, place.lines)],
    ):
        copies = [send(number + i, target) for i, target in enumerate(targets)]
        for copy in copies:
            copy.wait()
        for i in range(len(targets)):
            values[...] = values[...] + buffers[number + i]
        number += len(targets)


def scatter_kernel(sizes, *refs):
    grads, refs = refs[:4], refs[4:]
    (sums_in, *results), refs = refs[:3], refs[3:]
    outs, refs = refs[:4], refs[4:]
    (sums, *placed), refs = refs[:3], refs[3:]
    buffers, refs = refs[: 6 * 8], refs[6 * 8 :]
    sum_buffers, send, recv, local_sems = refs
    place = Place(*sizes)
    tp = place.tp_size
    greet_all(place)
    pieces = []
    for p, (g, part, parts) in enumerate(((0, 0, 1), (1, 0, 1), (2, 0, 2), (2, 1, 2), (3, 0, 2), (3, 1, 2))):
        per_core = grads[g].shape[-1] // tp
        width = per_core // parts
        out = outs[g].at[:, :, :, pl.ds(part * width, width)]
        pieces.append((grads[g], part * width, width, per_core, out) + tuple(buffers[8 * p : 8 * p + 8]))
    pieces = [pieces[p] for p in (4, 5, 2, 3, 1, 0)]
    scatter = Scatter(place, pieces, (send, recv), local_sems)
    sums[...] = sums_in[...]
    exchanges = []
    extra, half = len(pieces) * scatter.width, place.half
    for number, (own, whole) in enumerate(zip(results, placed)):
        exchanges.append(copy_to(own.at[1 - half], whole.at[half], (send, recv), extra + number, place.to_half))
        exchanges.append(pltpu.make_async_copy(own.at[half], whole.at[half], local_sems.at[len(pieces) + number]))
    for copy in exchanges:
        copy.start()
    for slot in range(len(pieces) + scatter.stages() - 1):
        for p in range(len(pieces)):
            if 0 <= slot - p < scatter.stages():
                scatter.stage(p, slot - p)
        if slot == 1:
            all_sum(place, sums, sum_buffers, (send, recv), extra + 2)
    for copy in exchanges:
        copy.wait()
    scatter.finish()


def scatter_all(mesh, grad_qkv, grad_out, grad_one, grad_two, sums, outputs, input_grad):
    fsdp, ctx, tp = (mesh.shape[name] for name in ("fsdp", "ctx", "tp"))
    lines = fsdp // 2
    rows = grad_one.shape[-2] // (8 * lines)

    def split(grad):
        return grad.reshape(grad.shape[:1] + (lines, 2, 2, 2, rows, grad.shape[-1]))

    grads = [split(grad) for grad in (grad_qkv, grad_out, grad_one, grad_two)]

    def part(grad):
        return jax.ShapeDtypeStruct((grad.shape[0], 2, rows, grad.shape[-1] // tp), F32)

    scratch = []
    for lead, width in (
        (3, grad_qkv.shape[-1] // tp),
        (1, grad_out.shape[-1] // tp),
        (1, grad_one.shape[-1] // tp // 2),
        (1, grad_one.shape[-1] // tp // 2),
        (1, grad_two.shape[-1] // tp // 2),
        (1, grad_two.shape[-1] // tp // 2),
    ):
        scratch += Scatter.buffers(lead, lines, tp, rows, width)
    arrivals = tp - 1 + 2 + lines - 1
    count = 6 * Scatter.slots(lines, tp) + arrivals + 2
    vmem, hbm = pl.BlockSpec(memory_space=pltpu.VMEM), pl.BlockSpec(memory_space=pl.ANY)
    found = pl.pallas_call(
        functools.partial(scatter_kernel, (fsdp, ctx, tp)),
        name="scatter_gradients",
        out_shape=[part(grad) for grad in grads]
        + [jax.ShapeDtypeStruct(sums.shape, F32)]
        + [jax.ShapeDtypeStruct(outputs.shape, BF)] * 2,
        in_specs=[hbm] * 4 + [vmem] * 3,
        out_specs=[vmem] * 5 + [hbm] * 2,
        scratch_shapes=scratch
        + [
            pltpu.VMEM((arrivals,) + sums.shape, F32),
            pltpu.SemaphoreType.DMA((count,)),
            pltpu.SemaphoreType.DMA((count,)),
            pltpu.SemaphoreType.DMA((8,)),
        ],
        compiler_params=pltpu.CompilerParams(collective_id=1, has_side_effects=True, vmem_limit_bytes=67043328),
    )(*grads, sums, outputs, input_grad)
    return [one.reshape(one.shape[0], 2 * rows, one.shape[-1]) for one in found[:4]] + list(found[4:])


SEQ_LEN = 577
HD = 64


def normalize_rows(values, gain_row, shift_row):
    average = jnp.mean(values, axis=-1, keepdims=True)
    centred = values - average
    inv_std = lax.rsqrt(jnp.mean(centred * centred, axis=-1, keepdims=True) + 1e-05)
    normed = centred * inv_std
    return normed, inv_std, normed * gain_row + shift_row


def normalize_back(upstream, normed, inv_std, gain_row):
    scaled = upstream * gain_row
    inner = (
        scaled
        - jnp.mean(scaled, axis=-1, keepdims=True)
        - normed * jnp.mean(scaled * normed, axis=-1, keepdims=True)
    )
    return inv_std * inner


def dot(form, left, right):
    return jnp.einsum(form, left, right, preferred_element_type=F32)


def body(mesh, inputs, cotangent, slot_mask, key_mask, ln1_gain, ln1_bias, w_qkv, b_qv, w_out, b_out, ln2_gain, ln2_bias, w_fc1, b_fc1, w_fc2, b_fc2):
    fsdp, ctx, tp = (mesh.shape[name] for name in ("fsdp", "ctx", "tp"))
    width = inputs.shape[-1]
    seq = inputs.shape[2] * ctx
    heads = width // HD
    half, core = lax.axis_index("ctx"), lax.axis_index("tp")
    vectors = (ln1_gain, ln1_bias, ln2_gain, ln2_bias, b_out, b_fc2, b_qv, b_fc1)
    small = jnp.concatenate([vector.reshape(-1) for vector in vectors]).astype(F32)
    small = jnp.pad(small, (0, -small.size % 1024)).reshape(-1, 128)
    found = gather_all(
        mesh, (w_qkv.transpose(1, 0, 2), w_out.T, w_fc1, w_fc2.T), inputs[:, 0], cotangent[:, 0], small
    )
    m_qkv, m_out, m_one, m_two, tokens, cotangents, all_small = found
    tokens, cotangents = tokens.reshape(seq, width), cotangents.reshape(seq, width)
    all_small = all_small.reshape(tp, fsdp, -1)
    whole, place = [], 0
    for vector in vectors:
        part = all_small[:, :, place : place + vector.size].reshape((tp, fsdp) + vector.shape)
        place += vector.size
        if vector.ndim == 1:
            whole.append(part[0].reshape(-1))
        elif vector.ndim == 2:
            whole.append(part.transpose(0, 2, 1, 3).reshape(-1))
        else:
            whole.append(part.transpose(2, 0, 3, 1, 4).reshape(2, -1))
    gain_one, shift_one, gain_two, shift_two, bias_out, bias_fc2, bias_qv, bias_fc1 = whole
    keys_ok = lax.dynamic_slice(key_mask, (half, core, 0), (1, 1, seq)).reshape(seq) > 0
    slot_ok = lax.dynamic_slice(slot_mask, (half, 0), (1, 1)).reshape(()) > 0
    rows_ok = ((jnp.arange(seq) < SEQ_LEN) & slot_ok).astype(F32)[:, None]

    rows_in = tokens.astype(F32)
    normed_one, inv_one, scaled_one = normalize_rows(rows_in, gain_one, shift_one)
    low_one = scaled_one.astype(BF)
    query = (dot("rd,de->re", low_one, m_qkv[0]) + bias_qv[0]).astype(BF).reshape(seq, heads, HD)
    keys = dot("rd,de->re", low_one, m_qkv[1]).astype(BF).reshape(seq, heads, HD)
    values = (dot("rd,de->re", low_one, m_qkv[2]) + bias_qv[1]).astype(BF).reshape(seq, heads, HD)
    scores = jnp.where(keys_ok[None, None, :], dot("qhd,khd->hqk", query, keys) * 0.125, -jnp.inf)
    row_max = jnp.max(scores, axis=-1, keepdims=True)
    lifted = jnp.exp(scores - row_max)
    row_sum = jnp.sum(lifted, axis=-1, keepdims=True)
    soft = lifted / row_sum
    soft_low = soft.astype(BF)
    mixed = dot("hqk,khd->qhd", soft_low, values).astype(BF).reshape(seq, width)
    hidden_one = rows_in + dot("re,de->rd", mixed, m_out) + bias_out
    normed_two, inv_two, scaled_two = normalize_rows(hidden_one, gain_two, shift_two)
    low_two = scaled_two.astype(BF)
    before = dot("rd,df->rf", low_two, m_one) + bias_fc1
    gate = jax.nn.sigmoid(1.702 * before)
    active = (before * gate).astype(BF)
    outputs = ((hidden_one + dot("rf,df->rd", active, m_two) + bias_fc2) * rows_ok).astype(BF)

    grad_out = cotangents.astype(F32) * rows_ok
    grad_low = grad_out.astype(BF)
    grad_two_matrix = dot("rd,rf->df", grad_low, active).astype(BF)
    grad_active = dot("rd,df->rf", grad_low, m_two)
    grad_before = (grad_active * (gate + 1.702 * before * gate * (1.0 - gate))).astype(BF)
    grad_one_matrix = dot("rd,rf->df", low_two, grad_before).astype(BF)
    grad_two = dot("rf,df->rd", grad_before, m_one)
    grad_hidden = grad_out + normalize_back(grad_two, normed_two, inv_two, gain_two)
    hidden_low = grad_hidden.astype(BF)
    grad_out_matrix = dot("rd,re->de", hidden_low, mixed).astype(BF)
    grad_mixed = dot("rd,de->re", hidden_low, m_out).astype(BF).reshape(seq, heads, HD)
    grad_soft = dot("qhd,khd->hqk", grad_mixed, values)
    inner_sum = jnp.sum(grad_soft * soft, axis=-1, keepdims=True)
    grad_scores = (soft * (grad_soft - inner_sum)).astype(BF)
    grad_query = (dot("hqk,khd->qhd", grad_scores, keys) * 0.125).astype(BF).reshape(seq, width)
    grad_keys = (dot("hqk,qhd->khd", grad_scores, query) * 0.125).astype(BF).reshape(seq, width)
    grad_values = dot("hqk,qhd->khd", soft_low, grad_mixed).astype(BF).reshape(seq, width)
    grad_qkv_matrix = jnp.stack([dot("rd,re->de", low_one, g).astype(BF) for g in (grad_query, grad_keys, grad_values)])
    grad_one = (
        dot("re,de->rd", grad_query, m_qkv[0])
        + dot("re,de->rd", grad_keys, m_qkv[1])
        + dot("re,de->rd", grad_values, m_qkv[2])
    )
    input_grad = (grad_hidden + normalize_back(grad_one, normed_one, inv_one, gain_one)).astype(BF)

    def over_rows(values):
        return jnp.sum(values.astype(F32), axis=0)

    sums = [
        over_rows(grad_one * normed_one),
        over_rows(grad_one),
        over_rows(grad_two * normed_two),
        over_rows(grad_two),
        over_rows(grad_hidden),
        over_rows(grad_out),
        over_rows(grad_query),
        over_rows(grad_values),
        over_rows(grad_before),
    ]
    found = scatter_all(
        mesh,
        grad_qkv_matrix,
        grad_out_matrix[None],
        grad_one_matrix[None],
        grad_two_matrix[None],
        jnp.concatenate(sums).reshape(-1, 128),
        outputs.reshape(ctx, -1, width),
        input_grad.reshape(ctx, -1, width),
    )
    s_qkv, s_out, s_one, s_two, sums, outputs, input_grad = found
    sums = sums.reshape(-1)
    device = lax.axis_index("fsdp") * ctx + half
    per = width // (fsdp * ctx * tp)
    own = lax.dynamic_slice(sums[: 6 * width].reshape(6, width), (0, (device * tp + core) * per), (6, per))
    bias_sums = sums[6 * width : 8 * width].reshape(2, heads, HD)
    b_qv_grad = lax.dynamic_slice(
        bias_sums, (0, core * (heads // tp), device * (HD // (fsdp * ctx))), (2, heads // tp, HD // (fsdp * ctx))
    )
    fc1_sums = sums[8 * width :].reshape(-1, 64)
    b_fc1_grad = lax.dynamic_slice(
        fc1_sums, (core * (fc1_sums.shape[0] // tp), device * (64 // (fsdp * ctx))), (fc1_sums.shape[0] // tp, 64 // (fsdp * ctx))
    )
    return (
        outputs[:, None],
        input_grad[:, None],
        own[0],
        own[1],
        s_qkv.transpose(1, 0, 2),
        b_qv_grad,
        s_out[0].T,
        own[4],
        own[2],
        own[3],
        s_one[0],
        b_fc1_grad,
        s_two[0].T,
        own[5],
    )


def solution(mesh):
    in_specs = (
        P(None, ("fsdp", "tp"), "ctx", None),
        P(None, ("fsdp", "tp"), "ctx", None),
        P(None, ("fsdp", "tp")),
        P(None, "fsdp", None),
        P("fsdp"),
        P("fsdp"),
        P("fsdp", None, "tp"),
        P(None, "tp", "fsdp"),
        P("tp", "fsdp"),
        P("fsdp"),
        P("fsdp"),
        P("fsdp"),
        P("fsdp", "tp"),
        P("tp", "fsdp"),
        P("tp", "fsdp"),
        P("fsdp"),
    )
    out_specs = (
        P(None, ("fsdp", "tp"), "ctx", None),
        P(None, ("fsdp", "tp"), "ctx", None),
        P(("fsdp", "ctx", "tp")),
        P(("fsdp", "ctx", "tp")),
        P(("fsdp", "ctx"), None, "tp"),
        P(None, "tp", ("fsdp", "ctx")),
        P("tp", ("fsdp", "ctx")),
        P(("fsdp", "ctx", "tp")),
        P(("fsdp", "ctx", "tp")),
        P(("fsdp", "ctx", "tp")),
        P(("fsdp", "ctx"), "tp"),
        P("tp", ("fsdp", "ctx")),
        P("tp", ("fsdp", "ctx")),
        P(("fsdp", "ctx", "tp")),
    )
    return jax.shard_map(
        functools.partial(body, mesh), mesh=mesh, in_specs=in_specs, out_specs=out_specs, check_vma=False
    )
```
